32 devices in a mesh: segment: 4 (over y, x), tp: 8 (over z, core).
Axes of the slice: x: 2, y: 2, z: 4, core: 2. Of those that a mesh axis runs over, the one named last changes fastest.
Arguments:
- memory: bfloat16 [512, 4096], P('segment', 'tp'), may hold values from -6 to 6
- norm_gain: float32 [4096], replicated, may hold values from 0.1 to 1.9
- queries: bfloat16 [4, 1024, 4096], P('segment', None, 'tp'), may hold values from -200 to 200
- key_weight: bfloat16 [4, 4096, 4096], P('segment', None, 'tp'), may hold values from -0.09375 to 0.09375
- value_weight: bfloat16 [4, 4096, 4096], P('segment', None, 'tp'), may hold values from -0.09375 to 0.09375
- context_grad: bfloat16 [4, 1024, 4096], P('segment', None, 'tp'), may hold values from -6 to 6
Outputs:
- context: bfloat16 [4, 1024, 4096], P('segment', None, 'tp')
- query_grad: bfloat16 [4, 1024, 4096], P('segment', None, 'tp')
- key_weight_grad: float32 [4, 4096, 4096], P('segment', None, 'tp')
- value_weight_grad: float32 [4, 4096, 4096], P('segment', None, 'tp')
- encoder_output_gradient: float32 [512, 4096], P('segment', 'tp')
The draws below stay inside these ranges and needn't reach their ends.
All inputs are finite; a program needn't handle non-finite values.
Results may differ from the reference program's by a relative error of at most 0.015.
The reference program's roundings to bfloat16 on the way (of `normed`, `attend_low` and `grad_scores`) count: a program that leaves them out, or rounds other values in their place, can miss the bound.
Values may be sent and summed in bfloat16 or wider, within the bound.
A program may use at most 128 MiB of HBM per device.

```python
import jax
import jax.numpy as jnp
from jax import lax

D = 4096
HD = 256
HEADS = 16
TGT = 1024
SRC = 512
SECTIONS = 4
N_SEGMENT = 4


def draw_queries(key, part):
    base = jax.random.truncated_normal(jax.random.fold_in(key, 11), -6.0, 6.0, (N_SEGMENT, TGT, D), jnp.float32)
    return base.astype(jnp.bfloat16)


def block_levels(rng, dims, split, low, largest):
    gain = 1.0
    for axis_at, blocks in split:
        heights = jax.random.uniform(jax.random.fold_in(jax.random.fold_in(rng, 6), axis_at), (blocks,), jnp.float32, low / len(split), largest / len(split))
        gain = gain * jnp.repeat(jnp.exp(heights), dims[axis_at] // blocks).reshape((-1,) + (1,) * (len(dims) - 1 - axis_at))
    return gain


def centred(own_key, dims, scale, limit, shards=(), dtype=jnp.bfloat16):
    factor_of = block_levels(own_key, dims, shards, -0.22, 0.18) if shards else 1.0
    result = jax.random.normal(own_key, dims, jnp.float32) * scale * factor_of
    return jnp.minimum(jnp.maximum(result, -limit), limit).astype(dtype)


def setup_inputs(seed: int = 0) -> dict:
    arg_keys = jax.random.split(jax.random.key(seed), 7)
    memory = centred(arg_keys[0], (SRC, D), 1.0, 6.0, ((0, 4), (1, 8)))
    norm_gain = jnp.clip(1.0 + 0.18 * jax.random.normal(arg_keys[1], (D,), jnp.float32), 0.1, 1.9)
    queries = draw_queries(jax.random.fold_in(arg_keys[6], 71), 0)
    key_weight = centred(arg_keys[3], (SECTIONS, D, D), D ** -0.5, 0.09375, ((0, 4), (2, 8)))
    value_weight = centred(arg_keys[4], (SECTIONS, D, D), D ** -0.5, 0.09375, ((0, 4), (2, 8)))
    context_grad = centred(arg_keys[5], (SECTIONS, TGT, D), 1.0, 6.0, ((0, 4), (2, 8)))
    return dict(memory=memory, norm_gain=norm_gain, queries=queries, key_weight=key_weight, value_weight=value_weight, context_grad=context_grad)


def section_pass(normed, items):
    query_rows, key_mat, value_mat, dctx = items
    key_rows = jnp.dot(normed, key_mat, preferred_element_type=jnp.float32).astype(jnp.bfloat16)
    value_rows = jnp.dot(normed, value_mat, preferred_element_type=jnp.float32).astype(jnp.bfloat16)
    scale = HD ** (-0.5)
    qh = query_rows.reshape(TGT, HEADS, HD).astype(jnp.float32)
    kh = key_rows.reshape(SRC, HEADS, HD).astype(jnp.float32)
    vh = value_rows.reshape(SRC, HEADS, HD).astype(jnp.float32)
    dch = dctx.reshape(TGT, HEADS, HD).astype(jnp.float32)
    scores = jnp.einsum('qhd,khd->hqk', qh, kh) * scale
    maxima = lax.optimization_barrier(jnp.max(scores, axis=-1, keepdims=True))
    exponent = jnp.exp(scores - maxima)
    attend = exponent / lax.optimization_barrier(jnp.sum(exponent, axis=-1, keepdims=True))
    attend_low = attend.astype(jnp.bfloat16)
    context = jnp.einsum('hqk,khd->qhd', attend_low.astype(jnp.float32), vh).astype(jnp.bfloat16)
    grad_attend = jnp.einsum('qhd,khd->hqk', dch, vh)
    row_dots = lax.optimization_barrier(jnp.sum(grad_attend * attend, axis=-1, keepdims=True))
    grad_scores = (attend * (grad_attend - row_dots) * scale).astype(jnp.bfloat16).astype(jnp.float32)
    query_grad = jnp.einsum('hqk,khd->qhd', grad_scores, kh).astype(jnp.bfloat16)
    grad_keys = jnp.einsum('hqk,qhd->khd', grad_scores, qh).astype(jnp.bfloat16).reshape(SRC, D)
    grad_values = jnp.einsum('hqk,qhd->khd', attend_low.astype(jnp.float32), dch).astype(jnp.bfloat16).reshape(SRC, D)
    key_grad = jnp.dot(normed.T, grad_keys, preferred_element_type=jnp.float32)
    value_grad = jnp.dot(normed.T, grad_values, preferred_element_type=jnp.float32)
    grad_normed = jnp.dot(grad_keys, key_mat.T, preferred_element_type=jnp.float32)
    grad_normed = grad_normed + jnp.dot(grad_values, value_mat.T, preferred_element_type=jnp.float32)
    return (context.reshape(TGT, D), query_grad.reshape(TGT, D), key_grad, value_grad, grad_normed)

def reference(memory, norm_gain, queries, key_weight, value_weight, context_grad):
    encoder_states = memory.astype(jnp.float32)
    row_inverse_scale = lax.rsqrt(lax.optimization_barrier(jnp.mean(encoder_states * encoder_states, axis=1)) + 1e-06)
    normed = (encoder_states * row_inverse_scale[:, None] * norm_gain).astype(jnp.bfloat16)
    context, query_grad, key_grad, value_grad, grad_parts = lax.map(lambda items: section_pass(normed, items), (queries, key_weight, value_weight, context_grad))
    grad_normed = lax.optimization_barrier(jnp.sum(grad_parts, axis=0))
    upper_term = grad_normed * norm_gain
    centered_normalized = encoder_states * row_inverse_scale[:, None]
    row_average = lax.optimization_barrier(jnp.mean(upper_term * centered_normalized, axis=1))
    encoder_output_gradient = row_inverse_scale[:, None] * (upper_term - centered_normalized * row_average[:, None])
    return (context, query_grad, key_grad, value_grad, encoder_output_gradient)
```

```python
import functools

import jax
import jax.numpy as jnp
from jax import lax
from jax.experimental import pallas as pl
from jax.experimental.pallas import tpu as pltpu
from jax.sharding import PartitionSpec as P

HD = 256
EPS = 1e-06
F32 = jnp.float32
BF16 = jnp.bfloat16
MESH = pl.DeviceIdType.MESH
VM = pltpu.VMEM
DMA = pltpu.SemaphoreType.DMA


def bits_of(n):
    return n.bit_length() - 1


def orders(n):
    up = list(range(bits_of(n)))
    return up, up[::-1]


def greet(n_seg, n_tp, s, t):
    barrier = pltpu.get_barrier_semaphore()
    count = 0
    for b in range(bits_of(n_seg)):
        pl.semaphore_signal(barrier, inc=1, device_id=(s ^ (1 << b), t), device_id_type=MESH)
        count += 1
    for m in range(1, n_tp):
        pl.semaphore_signal(barrier, inc=1, device_id=(s, t ^ m), device_id_type=MESH)
        count += 1
    pl.semaphore_wait(barrier, count)


def remote(src, dst, tx, rx, device):
    return pltpu.make_async_remote_copy(
        src_ref=src, dst_ref=dst, send_sem=tx, recv_sem=rx, device_id=device, device_id_type=MESH
    )


def sum_over_tp(n_tp, s, t, row_sums, mine, slots, tx, rx):
    rows = row_sums.shape[0]
    mine[...] = jnp.broadcast_to(row_sums, (rows, rows)).T[:8]
    copies = []
    for m in range(1, n_tp):
        c = remote(mine, slots.at[m], tx.at[m], rx.at[m], (s, t ^ m))
        c.start()
        copies.append(c)
    total = mine[...]
    for m in range(1, n_tp):
        copies[m - 1].wait()
        total = total + slots[m]
    return jnp.broadcast_to(total[:1], (rows, rows)).T[:, :1]


def gather_kernel(
    n_seg, n_tp, mem_ref, gain_ref, wk_hbm, wv_hbm,
    normed_hbm, k_ref, v_ref, scale_ref,
    buf, wk, wv, kacc, vacc, mine, slots,
    w_sem, sq_tx, sq_rx, z_tx, z_rx, seg_tx, seg_rx, sib_tx, sib_rx, out_sem,
):
    s = lax.axis_index("segment")
    t = lax.axis_index("tp")
    rows, cols = mem_ref.shape
    half = rows // 2
    n_z = n_tp // 2
    hidden = n_tp * cols
    load_k = pltpu.make_async_copy(wk_hbm, wk, w_sem.at[0])
    load_v = pltpu.make_async_copy(wv_hbm, wv, w_sem.at[1])
    load_k.start()
    load_v.start()
    greet(n_seg, n_tp, s, t)
    x = mem_ref[...].astype(F32)
    squares = sum_over_tp(
        n_tp, s, t, jnp.sum(x * x, axis=1, keepdims=True), mine, slots, sq_tx, sq_rx
    )
    scale = lax.rsqrt(squares / hidden + EPS)
    scale_ref[...] = jnp.broadcast_to(scale, scale_ref.shape)
    own = pl.ds(pl.multiple_of(s * rows, rows), rows)
    buf[t, own, :] = (x * scale * gain_ref[t]).astype(BF16)
    kacc[...] = jnp.zeros_like(kacc)
    vacc[...] = jnp.zeros_like(vacc)

    def block(m):
        return t ^ (m * 2)

    def piece(m, h, mask):
        start = pl.multiple_of((s ^ mask) * rows + h * half, half)
        return buf.at[block(m), pl.ds(start, half), :]

    def seg_copy(m, h, mask, b):
        ref = piece(m, h, mask)
        return remote(
            ref, ref, seg_tx.at[m, h, mask, b], seg_rx.at[m, h, mask ^ (1 << b)], (s ^ (1 << b), t)
        )

    def seg_arrival(m, h, mask):
        ref = piece(m, h, mask)
        b = bits_of(n_seg) - 1
        return remote(ref, ref, seg_tx.at[m, h, 0, b], seg_rx.at[m, h, mask], (s ^ (1 << b), t))

    def z_copy(m):
        ref = buf.at[t, own, :]
        return remote(ref, ref, z_tx.at[m], z_rx.at[m], (s, t ^ (m * 2)))

    def z_arrival(m):
        ref = buf.at[block(m), own, :]
        return remote(ref, ref, z_tx.at[m], z_rx.at[m], (s, t ^ (m * 2)))

    def sib_copy(m):
        ref = buf.at[block(m)]
        return remote(ref, ref, sib_tx.at[m], sib_rx.at[m], (s, t ^ 1))

    def sib_arrival(m):
        ref = buf.at[block(m) ^ 1]
        return remote(ref, ref, sib_tx.at[m], sib_rx.at[m], (s, t ^ 1))

    def out_copy(b, i):
        return pltpu.make_async_copy(buf.at[b], normed_hbm.at[b], out_sem.at[i])

    relayed = []
    for h, order in enumerate(orders(n_seg)):
        have = [0]
        for b in order:
            for mask in have:
                if mask:
                    relayed.append((h, mask, b))
            have = have + [mask ^ (1 << b) for mask in have]
    waited = []
    for h, mask, _ in relayed:
        if (h, mask) not in waited:
            waited.append((h, mask))

    def first_sends(m):
        for h in range(2):
            for b in orders(n_seg)[h]:
                seg_copy(m, h, 0, b).start()

    def relay(m):
        seen = []
        for h, mask, b in relayed:
            if (h, mask) not in seen:
                seg_arrival(m, h, mask).wait_recv()
                seen.append((h, mask))
            seg_copy(m, h, mask, b).start()

    def project(b):
        rows_w = pl.ds(pl.multiple_of(b * cols, cols), cols)
        kacc[...] += jnp.dot(buf[b], wk[rows_w, :], preferred_element_type=F32)
        vacc[...] += jnp.dot(buf[b], wv[rows_w, :], preferred_element_type=F32)

    first_sends(0)
    for m in range(1, n_z):
        z_copy(m).start()

    @pl.loop(0, n_z + 2)
    def _(i):
        @pl.when(i + 1 < n_z)
        def _():
            z_arrival(i + 1).wait_recv()
            first_sends(i + 1)

        @pl.when(i < n_z)
        def _():
            relay(i)

        @pl.when(i == 1)
        def _():
            load_k.wait()
            load_v.wait()

        @pl.when((i >= 1) & (i <= n_z))
        def _():
            m = i - 1
            for h in range(2):
                for mask in range(1, n_seg):
                    if (h, mask) not in waited:
                        seg_arrival(m, h, mask).wait_recv()
            sib_copy(m).start()
            out_copy(block(m), m).start()

        @pl.when(i >= 2)
        def _():
            sib_arrival(i - 2).wait_recv()
            out_copy(block(i - 2) ^ 1, i - 2 + n_z).start()

        @pl.loop(jnp.where(i == 0, 2, jnp.where(i == 1, 1, 0)), jnp.where(i == n_z + 1, 1, jnp.where(i == 0, 2, 2)))
        def _(j):
            project(block(i - 2 + j) ^ (1 - j))

    k_ref[...] = kacc[...].astype(BF16)
    v_ref[...] = vacc[...].astype(BF16)
    for m in range(1, n_z):
        z_copy(m).wait_send()

    @pl.loop(0, n_z)
    def _(m):
        for h in range(2):
            for b in orders(n_seg)[h]:
                seg_copy(m, h, 0, b).wait_send()
        for h, mask, b in relayed:
            seg_copy(m, h, mask, b).wait_send()
        sib_copy(m).wait_send()
        out_copy(block(m), m).wait()
        out_copy(block(m) ^ 1, m + n_z).wait()


def gather(n_seg, n_tp, memory, gain, wk, wv):
    rows, cols = memory.shape
    n_z = n_tp // 2
    nb = bits_of(n_seg)
    vmem = pl.BlockSpec(memory_space=pltpu.VMEM)
    anyw = pl.BlockSpec(memory_space=pl.ANY)
    src = n_seg * rows
    return pl.pallas_call(
        functools.partial(gather_kernel, n_seg, n_tp),
        out_shape=(
            jax.ShapeDtypeStruct((n_tp, src, cols), BF16),
            jax.ShapeDtypeStruct((src, cols), BF16),
            jax.ShapeDtypeStruct((src, cols), BF16),
            jax.ShapeDtypeStruct((rows, 128), F32),
        ),
        in_specs=[vmem, vmem, anyw, anyw],
        out_specs=(anyw, vmem, vmem, vmem),
        scratch_shapes=[
            VM((n_tp, src, cols), BF16),
            VM(wk.shape, BF16),
            VM(wv.shape, BF16),
            VM((src, cols), F32),
            VM((src, cols), F32),
            VM((8, rows), F32),
            VM((n_tp, 8, rows), F32),
            DMA((2,)),
            DMA((n_tp,)),
            DMA((n_tp,)),
            DMA((n_z,)),
            DMA((n_z,)),
            DMA((n_z, 2, n_seg, nb)),
            DMA((n_z, 2, n_seg)),
            DMA((n_z,)),
            DMA((n_z,)),
            DMA((n_tp,)),
        ],
        compiler_params=pltpu.CompilerParams(collective_id=0, has_side_effects=True),
        name="gather_project",
    )(memory, gain, wk, wv)


def attention_kernel(q_ref, k_ref, v_ref, d_ref, c_ref, qg_ref, gk_ref, gv_ref, gk_acc, gv_acc):
    i = pl.program_id(1)
    scale = HD ** (-0.5)
    nt = (((1,), (1,)), ((), ()))
    tn = (((0,), (0,)), ((), ()))
    q, k, v, d = q_ref[...], k_ref[...], v_ref[...], d_ref[...]
    scores = lax.dot_general(q, k, nt, preferred_element_type=F32) * scale
    grad_attend = lax.dot_general(d, v, nt, preferred_element_type=F32)
    exponent = jnp.exp(scores - jnp.max(scores, axis=-1, keepdims=True))
    attend = exponent * (1.0 / jnp.sum(exponent, axis=-1, keepdims=True))
    attend_low = attend.astype(BF16)
    row_dots = jnp.sum(grad_attend * attend, axis=-1, keepdims=True)
    grad_scores = (attend * (grad_attend - row_dots) * scale).astype(BF16)
    c_ref[...] = jnp.dot(attend_low, v, preferred_element_type=F32).astype(BF16)
    qg_ref[...] = jnp.dot(grad_scores, k, preferred_element_type=F32).astype(BF16)
    gk = lax.dot_general(grad_scores, q, tn, preferred_element_type=F32)
    gv = lax.dot_general(attend_low, d, tn, preferred_element_type=F32)

    @pl.when(i == 0)
    def _():
        gk_acc[...] = gk
        gv_acc[...] = gv

    @pl.when(i > 0)
    def _():
        gk_acc[...] += gk
        gv_acc[...] += gv

    @pl.when(i == pl.num_programs(1) - 1)
    def _():
        gk_ref[...] = gk_acc[...].astype(BF16)
        gv_ref[...] = gv_acc[...].astype(BF16)


def attention(q, k, v, d):
    tgt, cols = q.shape
    src = k.shape[0]
    tile = 256
    tspec = pl.BlockSpec((tile, HD), lambda h, i: (i, h))
    sspec = pl.BlockSpec((src, HD), lambda h, i: (0, h))
    return pl.pallas_call(
        attention_kernel,
        grid=(cols // HD, tgt // tile),
        out_shape=(
            jax.ShapeDtypeStruct((tgt, cols), BF16),
            jax.ShapeDtypeStruct((tgt, cols), BF16),
            jax.ShapeDtypeStruct((src, cols), BF16),
            jax.ShapeDtypeStruct((src, cols), BF16),
        ),
        in_specs=[tspec, sspec, sspec, tspec],
        out_specs=(tspec, tspec, sspec, sspec),
        scratch_shapes=[VM((src, HD), F32), VM((src, HD), F32)],
        name="attention",
    )(q, k, v, d)


def weight_grad_kernel(n_ref, gk_ref, gv_ref, kg_ref, vg_ref):
    tn = (((0,), (0,)), ((), ()))
    kg_ref[...] = lax.dot_general(n_ref[...], gk_ref[...], tn, preferred_element_type=F32)
    vg_ref[...] = lax.dot_general(n_ref[...], gv_ref[...], tn, preferred_element_type=F32)


def weight_grads(normed, gk, gv):
    n_tp, src, cols = normed.shape
    full = pl.BlockSpec((src, cols), lambda i: (0, 0))
    out = pl.BlockSpec((cols, cols), lambda i: (i, 0))
    return pl.pallas_call(
        weight_grad_kernel,
        grid=(n_tp,),
        out_shape=(jax.ShapeDtypeStruct((n_tp * cols, cols), F32),) * 2,
        in_specs=[pl.BlockSpec((None, src, cols), lambda i: (i, 0, 0)), full, full],
        out_specs=(out, out),
        name="weight_grads",
    )(normed, gk, gv)


def scatter_kernel(
    n_seg, n_tp, gk_ref, gv_ref, wk_hbm, wv_hbm, mem_ref, gain_ref, scale_ref,
    out_ref,
    wk, wv, sib_out, sib_in, own, seg_in, z_in, mine, slots,
    wk_sem, wv_sem, sq_tx, sq_rx, z_tx, z_rx, seg_tx, seg_rx, sib_tx, sib_rx,
):
    s = lax.axis_index("segment")
    t = lax.axis_index("tp")
    rows, cols = mem_ref.shape
    half = rows // 2
    n_z = n_tp // 2
    hidden = n_tp * cols
    nt = (((1,), (1,)), ((), ()))

    def block(i):
        return t ^ ((n_z - 1 - i) * 2)

    def load(b, i):
        r = pl.ds(pl.multiple_of(b * cols, cols), cols)
        return (
            pltpu.make_async_copy(wk_hbm.at[r, :], wk.at[i], wk_sem.at[i]),
            pltpu.make_async_copy(wv_hbm.at[r, :], wv.at[i], wv_sem.at[i]),
        )

    @pl.loop(0, n_z)
    def _(i):
        for j in range(2):
            for c in load(block(i) ^ (1 - j), i * 2 + j):
                c.start()

    greet(n_seg, n_tp, s, t)

    def product(i):
        return lax.dot_general(
            gk_ref[...], wk[i], nt, preferred_element_type=F32
        ) + lax.dot_general(gv_ref[...], wv[i], nt, preferred_element_type=F32)

    def sib_copy(i):
        return remote(sib_out.at[i], sib_in.at[i], sib_tx.at[i], sib_rx.at[i], (s, t ^ 1))

    def rows_of(mask, h):
        return pl.ds(pl.multiple_of((s ^ mask) * rows + h * half, half), half)

    def seg_copy(i, h, mask, b):
        return remote(
            own.at[i, rows_of(mask, h), :],
            seg_in.at[i, h, mask],
            seg_tx.at[i, h, mask],
            seg_rx.at[i, h, mask],
            (s ^ (1 << b), t),
        )

    def z_copy(i):
        m = n_z - 1 - i
        r = pl.ds(pl.multiple_of(s * rows, rows), rows)
        return remote(own.at[i, r, :], z_in.at[i], z_tx.at[i], z_rx.at[i], (s, t ^ (m * 2)))

    steps = []
    for j in range(bits_of(n_seg)):
        pair = []
        for order in orders(n_seg):
            done = sum(1 << b for b in order[:j])
            b = order[j]
            pair.append((b, [k for k in range(n_seg) if not (k & done) and (k >> b) & 1]))
        steps.append(pair)

    def send(i, j):
        for h in range(2):
            b, masks = steps[j][h]
            for mask in masks:
                seg_copy(i, h, mask, b).start()

    def receive(i, j):
        for h in range(2):
            b, masks = steps[j][h]
            for mask in masks:
                seg_copy(i, h, mask, b).wait_recv()
                r = rows_of(mask ^ (1 << b), h)
                own[i, r, :] = (
                    own[i, r, :].astype(F32) + seg_in[i, h, mask].astype(F32)
                ).astype(BF16)

    n_steps = len(steps)

    @pl.loop(0, n_z + 1)
    def _(i):
        @pl.when(i < n_z)
        def _():
            for c in load(block(i) ^ 1, i * 2):
                c.wait()
            sib_out[i] = product(i * 2).astype(BF16)
            sib_copy(i).start()

        @pl.when(i > 0)
        def _():
            k = i - 1
            for c in load(block(k), k * 2 + 1):
                c.wait()
            mine_part = product(k * 2 + 1)
            sib_copy(k).wait_recv()
            own[k] = (mine_part + sib_in[k].astype(F32)).astype(BF16)
            send(k, 0)

    @pl.loop(0, n_z + n_steps - 1)
    def _(i):
        for j in range(n_steps):
            k = i - j

            @pl.when((k >= 0) & (k < n_z))
            def _():
                receive(k, j)
                if j + 1 < n_steps:
                    send(k, j + 1)
                else:
                    @pl.when(k < n_z - 1)
                    def _():
                        z_copy(k).start()

    own_rows = pl.ds(pl.multiple_of(s * rows, rows), rows)
    total = own[n_z - 1, own_rows, :].astype(F32)
    for i in range(n_z - 1):
        z_copy(i).wait_recv()
        total = total + z_in[i].astype(F32)
    upper = total * gain_ref[t]
    scale = scale_ref[:, :1]
    xhat = mem_ref[...].astype(F32) * scale
    inner = sum_over_tp(
        n_tp, s, t, jnp.sum(upper * xhat, axis=1, keepdims=True), mine, slots, sq_tx, sq_rx
    )
    out_ref[...] = scale * (upper - xhat * (inner / hidden))

    for i in range(n_z - 1):
        z_copy(i).wait_send()

    @pl.loop(0, n_z)
    def _(i):
        sib_copy(i).wait_send()
        for j in range(n_steps):
            for h in range(2):
                b, masks = steps[j][h]
                for mask in masks:
                    seg_copy(i, h, mask, b).wait_send()


def scatter(n_seg, n_tp, gk, gv, wk, wv, memory, gain, scale):
    rows, cols = memory.shape
    n_z = n_tp // 2
    vmem = pl.BlockSpec(memory_space=pltpu.VMEM)
    anyw = pl.BlockSpec(memory_space=pl.ANY)
    src = n_seg * rows
    return pl.pallas_call(
        functools.partial(scatter_kernel, n_seg, n_tp),
        out_shape=jax.ShapeDtypeStruct((rows, cols), F32),
        in_specs=[vmem, vmem, anyw, anyw, vmem, vmem, vmem],
        out_specs=vmem,
        scratch_shapes=[
            VM((n_tp, cols, cols), BF16),
            VM((n_tp, cols, cols), BF16),
            VM((n_z, src, cols), BF16),
            VM((n_z, src, cols), BF16),
            VM((n_z, src, cols), BF16),
            VM((n_z, 2, n_seg, rows // 2, cols), BF16),
            VM((n_z, rows, cols), BF16),
            VM((8, rows), F32),
            VM((n_tp, 8, rows), F32),
            DMA((n_tp,)),
            DMA((n_tp,)),
            DMA((n_tp,)),
            DMA((n_tp,)),
            DMA((n_z,)),
            DMA((n_z,)),
            DMA((n_z, 2, n_seg)),
            DMA((n_z, 2, n_seg)),
            DMA((n_z,)),
            DMA((n_z,)),
        ],
        compiler_params=pltpu.CompilerParams(collective_id=1, has_side_effects=True),
        name="grad_scatter",
    )(gk, gv, wk, wv, memory, gain, scale)


def local(n_seg, n_tp, memory, norm_gain, queries, key_weight, value_weight, context_grad):
    wk, wv = key_weight[0], value_weight[0]
    gain = norm_gain.reshape(n_tp, 1, memory.shape[1])
    normed, key_rows, value_rows, scale = gather(n_seg, n_tp, memory, gain, wk, wv)
    context, query_grad, gk, gv = attention(queries[0], key_rows, value_rows, context_grad[0])
    key_grad, value_grad = weight_grads(normed, gk, gv)
    out = scatter(n_seg, n_tp, gk, gv, wk, wv, memory, gain, scale)
    return context[None], query_grad[None], key_grad[None], value_grad[None], out


def solution(mesh):
    section = P("segment", None, "tp")
    n_seg, n_tp = mesh.shape["segment"], mesh.shape["tp"]
    return jax.shard_map(
        functools.partial(local, n_seg, n_tp),
        mesh=mesh,
        in_specs=(P("segment", "tp"), P(), section, section, section, section),
        out_specs=(section, section, section, section, P("segment", "tp")),
        check_vma=False,
    )
```

```python
import functools

import jax
import jax.numpy as jnp
from jax import lax
from jax.experimental import pallas as pl
from jax.experimental.pallas import tpu as pltpu
from jax.sharding import PartitionSpec as P

HD = 256
EPS = 1e-06
F32 = jnp.float32
BF16 = jnp.bfloat16
MESH = pl.DeviceIdType.MESH
VM = pltpu.VMEM
DMA = pltpu.SemaphoreType.DMA


def bits_of(n):
    return n.bit_length() - 1


def orders(n):
    up = list(range(bits_of(n)))
    return up, up[::-1]


def greet(n_seg, n_tp, s, t):
    barrier = pltpu.get_barrier_semaphore()
    for m in range(1, n_seg):
        pl.semaphore_signal(barrier, inc=1, device_id=(s ^ m, t), device_id_type=MESH)
    for m in range(1, n_tp):
        pl.semaphore_signal(barrier, inc=1, device_id=(s, t ^ m), device_id_type=MESH)
    pl.semaphore_wait(barrier, n_seg + n_tp - 2)


def remote(src, dst, tx, rx, device):
    return pltpu.make_async_remote_copy(
        src_ref=src, dst_ref=dst, send_sem=tx, recv_sem=rx, device_id=device, device_id_type=MESH
    )


def to_lanes(column):
    rows = column.shape[0]
    return jnp.broadcast_to(column, (rows, rows)).T[:8]


def to_column(lanes):
    rows = lanes.shape[1]
    return jnp.broadcast_to(lanes[:1], (rows, rows)).T


def gather_kernel(
    n_seg, n_tp, mem_hbm, gain_ref, wk_hbm, wv_hbm,
    nt_hbm, k_ref, v_ref, scale_ref,
    buf, turned, wk, wv, kacc, vacc, mine, slots, scales, scol,
    mem_sem, w_sem, sq_tx, sq_rx, sc_tx, sc_rx, zr_tx, zl_tx, z_rx,
    seg_tx, seg_rx, sib_tx, sib_rx, out_sem,
):
    s = lax.axis_index("segment")
    t = lax.axis_index("tp")
    rows, cols = mem_hbm.shape
    half = rows // 2
    n_z = n_tp // 2
    hidden = n_tp * cols
    zi = t // 2
    core = t % 2
    own = pl.ds(pl.multiple_of(s * rows, rows), rows)
    load_m = pltpu.make_async_copy(mem_hbm, buf.at[t, own, :], mem_sem.at[0])
    load_k = pltpu.make_async_copy(wk_hbm, wk, w_sem.at[0])
    load_v = pltpu.make_async_copy(wv_hbm, wv, w_sem.at[1])
    load_m.start()
    load_k.start()
    load_v.start()

    few = jnp.minimum(zi, n_z - 1 - zi)

    def z_of(q):
        d = (q + 1) // 2
        near = jnp.where(q % 2 == 1, zi - d, zi + d)
        far = jnp.where(zi > n_z - 1 - zi, zi - (q - few), zi + (q - few))
        return jnp.where(q <= 2 * few, near, far)

    def block(q):
        return z_of(q) * 2 + core

    def piece(q, h, mask):
        start = pl.multiple_of((s ^ mask) * rows + h * half, half)
        return buf.at[block(q), pl.ds(start, half), :]

    def seg_copy(q, h, mask, b):
        ref = piece(q, h, mask)
        return remote(
            ref, ref, seg_tx.at[q, h, mask, b], seg_rx.at[q, h, mask ^ (1 << b)], (s ^ (1 << b), t)
        )

    def seg_arrival(q, h, mask):
        ref = piece(q, h, mask)
        b = bits_of(n_seg) - 1
        return remote(ref, ref, seg_tx.at[q, h, 0, b], seg_rx.at[q, h, mask], (s ^ (1 << b), t))

    def z_copy(z, to_right):
        ref = buf.at[z * 2 + core, own, :]
        if to_right:
            return remote(ref, ref, zr_tx.at[z], z_rx.at[z], (s, t + 2))
        return remote(ref, ref, zl_tx.at[z], z_rx.at[z], (s, t - 2))

    def z_each(q, act):
        z = z_of(q)

        @pl.when((z <= zi) & (zi + 1 < n_z))
        def _():
            act(z_copy(z, True))

        @pl.when((z >= zi) & (zi > 0))
        def _():
            act(z_copy(z, False))

    def z_arrival(q):
        z = z_of(q)
        ref = buf.at[z * 2 + core, own, :]
        return remote(ref, ref, zr_tx.at[z], z_rx.at[z], (s, t ^ 2))

    def sib_copy(q):
        ref = buf.at[block(q)]
        return remote(ref, ref, sib_tx.at[q], sib_rx.at[q], (s, t ^ 1))

    def sib_arrival(q):
        ref = buf.at[block(q) ^ 1]
        return remote(ref, ref, sib_tx.at[q], sib_rx.at[q], (s, t ^ 1))

    def out_copy(b):
        return pltpu.make_async_copy(turned.at[b], nt_hbm.at[b], out_sem.at[b])

    def sq_copy(m):
        return remote(mine, slots.at[m], sq_tx.at[m], sq_rx.at[m], (s, t ^ m))

    def sc_copy(m):
        return remote(scales.at[s], scales.at[s], sc_tx.at[m], sc_rx.at[m], (s ^ m, t))

    def sc_arrival(m):
        ref = scales.at[s ^ m]
        return remote(ref, ref, sc_tx.at[m], sc_rx.at[m], (s ^ m, t))

    relayed = []
    for h, order in enumerate(orders(n_seg)):
        have = [0]
        for b in order:
            for mask in have:
                if mask:
                    relayed.append((h, mask, b))
            have = have + [mask ^ (1 << b) for mask in have]
    waited = []
    for h, mask, _ in relayed:
        if (h, mask) not in waited:
            waited.append((h, mask))

    def first_sends(q):
        for h in range(2):
            for b in orders(n_seg)[h]:
                seg_copy(q, h, 0, b).start()

    def relay(q):
        seen = []
        for h, mask, b in relayed:
            if (h, mask) not in seen:
                seg_arrival(q, h, mask).wait_recv()
                seen.append((h, mask))
            seg_copy(q, h, mask, b).start()

    def project(b):
        rows_w = pl.ds(pl.multiple_of(b * cols, cols), cols)
        normed = (buf[b].astype(F32) * scol[:, :1] * gain_ref[b]).astype(BF16)
        turned[b] = normed.T
        out_copy(b).start()
        kacc[...] += jnp.dot(normed, wk[rows_w, :], preferred_element_type=F32)
        vacc[...] += jnp.dot(normed, wv[rows_w, :], preferred_element_type=F32)

    load_m.wait()
    greet(n_seg, n_tp, s, t)
    z_each(0, lambda c: c.start())
    first_sends(0)
    x = buf[t, own, :].astype(F32)
    mine[...] = to_lanes(jnp.sum(x * x, axis=1, keepdims=True))
    for m in range(1, n_tp):
        sq_copy(m).start()
    kacc[...] = jnp.zeros_like(kacc)
    vacc[...] = jnp.zeros_like(vacc)

    @pl.loop(0, n_z + 2)
    def _(i):
        @pl.when(i + 1 < n_z)
        def _():
            z_arrival(i + 1).wait_recv()
            z_each(i + 1, lambda c: c.start())
            first_sends(i + 1)

        @pl.when(i == 0)
        def _():
            total = mine[...]
            for m in range(1, n_tp):
                sq_copy(m).wait()
                total = total + slots[m]
            scales[s] = lax.rsqrt(total / hidden + EPS)
            for m in range(1, n_seg):
                sc_copy(m).start()

        @pl.when(i < n_z)
        def _():
            relay(i)

        @pl.when(i == 1)
        def _():
            for m in range(1, n_seg):
                sc_copy(m).wait_send()
                sc_arrival(m).wait_recv()
            for k in range(n_seg):
                scol[k * rows:(k + 1) * rows, :] = to_column(scales[k])[:, :128]
            load_k.wait()
            load_v.wait()

        @pl.when((i >= 1) & (i <= n_z))
        def _():
            for h in range(2):
                for mask in range(1, n_seg):
                    if (h, mask) not in waited:
                        seg_arrival(i - 1, h, mask).wait_recv()
            sib_copy(i - 1).start()

        @pl.when(i >= 2)
        def _():
            sib_arrival(i - 2).wait_recv()

        @pl.loop(jnp.where(i == 0, 2, jnp.where(i == 1, 1, 0)), jnp.where(i == n_z + 1, 1, 2))
        def _(j):
            project(block(i - 2 + j) ^ (1 - j))

    k_ref[...] = kacc[...].astype(BF16)
    v_ref[...] = vacc[...].astype(BF16)
    scale_ref[...] = scol[own, :]

    @pl.loop(0, n_z)
    def _(q):
        z_each(q, lambda c: c.wait_send())
        for h in range(2):
            for b in orders(n_seg)[h]:
                seg_copy(q, h, 0, b).wait_send()
        for h, mask, b in relayed:
            seg_copy(q, h, mask, b).wait_send()
        sib_copy(q).wait_send()
        out_copy(block(q)).wait()
        out_copy(block(q) ^ 1).wait()


def gather(n_seg, n_tp, memory, gain, wk, wv):
    rows, cols = memory.shape
    n_z = n_tp // 2
    nb = bits_of(n_seg)
    vmem = pl.BlockSpec(memory_space=pltpu.VMEM)
    anyw = pl.BlockSpec(memory_space=pl.ANY)
    src = n_seg * rows
    return pl.pallas_call(
        functools.partial(gather_kernel, n_seg, n_tp),
        out_shape=(
            jax.ShapeDtypeStruct((n_tp, cols, src), BF16),
            jax.ShapeDtypeStruct((src, cols), BF16),
            jax.ShapeDtypeStruct((src, cols), BF16),
            jax.ShapeDtypeStruct((rows, 128), F32),
        ),
        in_specs=[anyw, vmem, anyw, anyw],
        out_specs=(anyw, vmem, vmem, vmem),
        scratch_shapes=[
            VM((n_tp, src, cols), BF16),
            VM((n_tp, cols, src), BF16),
            VM(wk.shape, BF16),
            VM(wv.shape, BF16),
            VM((src, cols), F32),
            VM((src, cols), F32),
            VM((8, rows), F32),
            VM((n_tp, 8, rows), F32),
            VM((n_seg, 8, rows), F32),
            VM((src, 128), F32),
            DMA((1,)),
            DMA((2,)),
            DMA((n_tp,)),
            DMA((n_tp,)),
            DMA((n_seg,)),
            DMA((n_seg,)),
            DMA((n_z,)),
            DMA((n_z,)),
            DMA((n_z,)),
            DMA((n_z, 2, n_seg, nb)),
            DMA((n_z, 2, n_seg)),
            DMA((n_z,)),
            DMA((n_z,)),
            DMA((n_tp,)),
        ],
        compiler_params=pltpu.CompilerParams(collective_id=0, has_side_effects=True),
        name="gather_project",
    )(memory, gain, wk, wv)


def attention_kernel(q_ref, k_ref, v_ref, d_ref, c_ref, qg_ref, gk_ref, gv_ref, gk_acc, gv_acc):
    i = pl.program_id(1)
    scale = HD ** (-0.5)
    nt = (((1,), (1,)), ((), ()))
    tn = (((0,), (0,)), ((), ()))
    q, k, v, d = q_ref[...], k_ref[...], v_ref[...], d_ref[...]
    scores = lax.dot_general(q, k, nt, preferred_element_type=F32) * scale
    grad_attend = lax.dot_general(d, v, nt, preferred_element_type=F32)
    exponent = jnp.exp(scores - jnp.max(scores, axis=-1, keepdims=True))
    attend = exponent * (1.0 / jnp.sum(exponent, axis=-1, keepdims=True))
    attend_low = attend.astype(BF16)
    row_dots = jnp.sum(grad_attend * attend, axis=-1, keepdims=True)
    grad_scores = (attend * (grad_attend - row_dots) * scale).astype(BF16)
    c_ref[...] = jnp.dot(attend_low, v, preferred_element_type=F32).astype(BF16)
    qg_ref[...] = jnp.dot(grad_scores, k, preferred_element_type=F32).astype(BF16)
    gk = lax.dot_general(grad_scores, q, tn, preferred_element_type=F32)
    gv = lax.dot_general(attend_low, d, tn, preferred_element_type=F32)

    @pl.when(i == 0)
    def _():
        gk_acc[...] = gk
        gv_acc[...] = gv

    @pl.when(i > 0)
    def _():
        gk_acc[...] += gk
        gv_acc[...] += gv

    @pl.when(i == pl.num_programs(1) - 1)
    def _():
        gk_ref[...] = gk_acc[...].astype(BF16)
        gv_ref[...] = gv_acc[...].astype(BF16)


def attention(q, k, v, d):
    tgt, cols = q.shape
    src = k.shape[0]
    tile = 256
    tspec = pl.BlockSpec((tile, HD), lambda h, i: (i, h))
    sspec = pl.BlockSpec((src, HD), lambda h, i: (0, h))
    return pl.pallas_call(
        attention_kernel,
        grid=(cols // HD, tgt // tile),
        out_shape=(
            jax.ShapeDtypeStruct((tgt, cols), BF16),
            jax.ShapeDtypeStruct((tgt, cols), BF16),
            jax.ShapeDtypeStruct((src, cols), BF16),
            jax.ShapeDtypeStruct((src, cols), BF16),
        ),
        in_specs=[tspec, sspec, sspec, tspec],
        out_specs=(tspec, tspec, sspec, sspec),
        scratch_shapes=[VM((src, HD), F32), VM((src, HD), F32)],
        name="attention",
    )(q, k, v, d)


def weight_grad_kernel(n_ref, gk_ref, gv_ref, kg_ref, vg_ref):
    kg_ref[...] = jnp.dot(n_ref[...], gk_ref[...], preferred_element_type=F32)
    vg_ref[...] = jnp.dot(n_ref[...], gv_ref[...], preferred_element_type=F32)


def weight_grads(normed, gk, gv):
    n_tp, cols, src = normed.shape
    full = pl.BlockSpec((src, cols), lambda i: (0, 0))
    out = pl.BlockSpec((cols, cols), lambda i: (i, 0))
    return pl.pallas_call(
        weight_grad_kernel,
        grid=(n_tp,),
        out_shape=(jax.ShapeDtypeStruct((n_tp * cols, cols), F32),) * 2,
        in_specs=[pl.BlockSpec((None, cols, src), lambda i: (i, 0, 0)), full, full],
        out_specs=(out, out),
        name="weight_grads",
    )(normed, gk, gv)


def scatter_kernel(
    n_seg, n_tp, gk_ref, gv_ref, k_ref, v_ref, wk_hbm, wv_hbm, mem_ref, gain_ref, scale_ref,
    out_ref,
    wk, wv, sib_out, sib_in, own, seg_in, z_in, mine, slots, sums, parts,
    wk_sem, wv_sem, sq_tx, sq_rx, in_tx, in_rx, z_tx, z_rx, seg_tx, seg_rx, sib_tx, sib_rx,
):
    s = lax.axis_index("segment")
    t = lax.axis_index("tp")
    rows, cols = mem_ref.shape
    half = rows // 2
    n_z = n_tp // 2
    hidden = n_tp * cols
    nt = (((1,), (1,)), ((), ()))

    def block(i):
        return t ^ ((n_z - 1 - i) * 2)

    def load(b, i):
        r = pl.ds(pl.multiple_of(b * cols, cols), cols)
        return (
            pltpu.make_async_copy(wk_hbm.at[r, :], wk.at[i], wk_sem.at[i]),
            pltpu.make_async_copy(wv_hbm.at[r, :], wv.at[i], wv_sem.at[i]),
        )

    @pl.loop(0, n_z)
    def _(i):
        for j in range(2):
            for c in load(block(i) ^ (1 - j), i * 2 + j):
                c.start()

    greet(n_seg, n_tp, s, t)

    def sq_copy(m):
        return remote(mine, slots.at[m], sq_tx.at[m], sq_rx.at[m], (s, t ^ m))

    def in_copy(m):
        return remote(sums.at[s ^ m], parts.at[m], in_tx.at[m], in_rx.at[m], (s ^ m, t))

    for k in range(n_seg):
        r = slice(k * rows, (k + 1) * rows)
        both = gk_ref[r].astype(F32) * k_ref[r].astype(F32) + gv_ref[r].astype(F32) * v_ref[
            r
        ].astype(F32)
        mine[k] = to_lanes(jnp.sum(both, axis=1, keepdims=True))
    for m in range(1, n_tp):
        sq_copy(m).start()

    def product(i):
        return lax.dot_general(
            gk_ref[...], wk[i], nt, preferred_element_type=F32
        ) + lax.dot_general(gv_ref[...], wv[i], nt, preferred_element_type=F32)

    def sib_copy(i):
        return remote(sib_out.at[i], sib_in.at[i], sib_tx.at[i], sib_rx.at[i], (s, t ^ 1))

    def rows_of(mask, h):
        return pl.ds(pl.multiple_of((s ^ mask) * rows + h * half, half), half)

    def seg_copy(i, h, mask, b):
        return remote(
            own.at[i, rows_of(mask, h), :],
            seg_in.at[i, h, mask],
            seg_tx.at[i, h, mask],
            seg_rx.at[i, h, mask],
            (s ^ (1 << b), t),
        )

    def z_copy(i):
        m = n_z - 1 - i
        r = pl.ds(pl.multiple_of(s * rows, rows), rows)
        return remote(own.at[i, r, :], z_in.at[i], z_tx.at[i], z_rx.at[i], (s, t ^ (m * 2)))

    steps = []
    for j in range(bits_of(n_seg)):
        pair = []
        for order in orders(n_seg):
            done = sum(1 << b for b in order[:j])
            b = order[j]
            pair.append((b, [k for k in range(n_seg) if not (k & done) and (k >> b) & 1]))
        steps.append(pair)

    def send(i, j):
        for h in range(2):
            b, masks = steps[j][h]
            for mask in masks:
                seg_copy(i, h, mask, b).start()

    def receive(i, j):
        for h in range(2):
            b, masks = steps[j][h]
            for mask in masks:
                seg_copy(i, h, mask, b).wait_recv()
                r = rows_of(mask ^ (1 << b), h)
                own[i, r, :] = (
                    own[i, r, :].astype(F32) + seg_in[i, h, mask].astype(F32)
                ).astype(BF16)

    n_steps = len(steps)

    @pl.loop(0, n_z + n_steps + 1)
    def _(i):
        @pl.when(i < n_z)
        def _():
            for c in load(block(i) ^ 1, i * 2):
                c.wait()
            sib_out[i] = product(i * 2).astype(BF16)
            sib_copy(i).start()

        @pl.when((i > 0) & (i <= n_z))
        def _():
            k = i - 1
            for c in load(block(k), k * 2 + 1):
                c.wait()
            mine_part = product(k * 2 + 1)
            sib_copy(k).wait_recv()
            own[k] = (mine_part + sib_in[k].astype(F32)).astype(BF16)
            send(k, 0)

        @pl.when(i == 2)
        def _():
            total = mine[...]
            for m in range(1, n_tp):
                sq_copy(m).wait()
                total = total + slots[m]
            sums[...] = total
            for m in range(1, n_seg):
                in_copy(m).start()

        for j in range(n_steps):
            k = i - 2 - j

            @pl.when((k >= 0) & (k < n_z))
            def _():
                receive(k, j)
                if j + 1 < n_steps:
                    send(k, j + 1)
                else:
                    @pl.when(k < n_z - 1)
                    def _():
                        z_copy(k).start()

    own_rows = pl.ds(pl.multiple_of(s * rows, rows), rows)
    total = own[n_z - 1, own_rows, :].astype(F32)
    for i in range(n_z - 1):
        z_copy(i).wait_recv()
        total = total + z_in[i].astype(F32)
    upper = total * gain_ref[t]
    scale = scale_ref[:, :1]
    xhat = mem_ref[...].astype(F32) * scale
    inner = sums[s]
    for m in range(1, n_seg):
        in_copy(m).wait()
        inner = inner + parts[m]
    inner = to_column(inner)[:, :1]
    out_ref[...] = scale * (upper - xhat * (inner / hidden))

    for i in range(n_z - 1):
        z_copy(i).wait_send()

    @pl.loop(0, n_z)
    def _(i):
        sib_copy(i).wait_send()
        for j in range(n_steps):
            for h in range(2):
                b, masks = steps[j][h]
                for mask in masks:
                    seg_copy(i, h, mask, b).wait_send()


def scatter(n_seg, n_tp, gk, gv, key_rows, value_rows, wk, wv, memory, gain, scale):
    rows, cols = memory.shape
    n_z = n_tp // 2
    vmem = pl.BlockSpec(memory_space=pltpu.VMEM)
    anyw = pl.BlockSpec(memory_space=pl.ANY)
    src = n_seg * rows
    return pl.pallas_call(
        functools.partial(scatter_kernel, n_seg, n_tp),
        out_shape=jax.ShapeDtypeStruct((rows, cols), F32),
        in_specs=[vmem, vmem, vmem, vmem, anyw, anyw, vmem, vmem, vmem],
        out_specs=vmem,
        scratch_shapes=[
            VM((n_tp, cols, cols), BF16),
            VM((n_tp, cols, cols), BF16),
            VM((n_z, src, cols), BF16),
            VM((n_z, src, cols), BF16),
            VM((n_z, src, cols), BF16),
            VM((n_z, 2, n_seg, rows // 2, cols), BF16),
            VM((n_z, rows, cols), BF16),
            VM((n_seg, 8, rows), F32),
            VM((n_tp, n_seg, 8, rows), F32),
            VM((n_seg, 8, rows), F32),
            VM((n_seg, 8, rows), F32),
            DMA((n_tp,)),
            DMA((n_tp,)),
            DMA((n_tp,)),
            DMA((n_tp,)),
            DMA((n_seg,)),
            DMA((n_seg,)),
            DMA((n_z,)),
            DMA((n_z,)),
            DMA((n_z, 2, n_seg)),
            DMA((n_z, 2, n_seg)),
            DMA((n_z,)),
            DMA((n_z,)),
        ],
        compiler_params=pltpu.CompilerParams(collective_id=1, has_side_effects=True),
        name="grad_scatter",
    )(gk, gv, key_rows, value_rows, wk, wv, memory, gain, scale)


def local(n_seg, n_tp, memory, norm_gain, queries, key_weight, value_weight, context_grad):
    wk, wv = key_weight[0], value_weight[0]
    gain = norm_gain.reshape(n_tp, 1, memory.shape[1])
    normed, key_rows, value_rows, scale = gather(n_seg, n_tp, memory, gain, wk, wv)
    context, query_grad, gk, gv = attention(queries[0], key_rows, value_rows, context_grad[0])
    key_grad, value_grad = weight_grads(normed, gk, gv)
    out = scatter(n_seg, n_tp, gk, gv, key_rows, value_rows, wk, wv, memory, gain, scale)
    return context[None], query_grad[None], key_grad[None], value_grad[None], out


def solution(mesh):
    section = P("segment", None, "tp")
    n_seg, n_tp = mesh.shape["segment"], mesh.shape["tp"]
    return jax.shard_map(
        functools.partial(local, n_seg, n_tp),
        mesh=mesh,
        in_specs=(P("segment", "tp"), P(), section, section, section, section),
        out_specs=(section, section, section, section, P("segment", "tp")),
        check_vma=False,
    )
```

```python
import functools

import jax
import jax.numpy as jnp
from jax import lax
from jax.experimental import pallas as pl
from jax.experimental.pallas import tpu as pltpu
from jax.sharding import PartitionSpec as P

HD = 256
EPS = 1e-06
F32 = jnp.float32
BF16 = jnp.bfloat16
MESH = pl.DeviceIdType.MESH
VM = pltpu.VMEM
DMA = pltpu.SemaphoreType.DMA


def bits_of(n):
    return n.bit_length() - 1


def orders(n):
    up = list(range(bits_of(n)))
    return up, up[::-1]


def greet(n_seg, n_tp, s, t):
    barrier = pltpu.get_barrier_semaphore()
    for m in range(1, n_seg):
        pl.semaphore_signal(barrier, inc=1, device_id=(s ^ m, t), device_id_type=MESH)
    for m in range(1, n_tp):
        pl.semaphore_signal(barrier, inc=1, device_id=(s, t ^ m), device_id_type=MESH)
    pl.semaphore_wait(barrier, n_seg + n_tp - 2)


def remote(src, dst, tx, rx, device):
    return pltpu.make_async_remote_copy(
        src_ref=src, dst_ref=dst, send_sem=tx, recv_sem=rx, device_id=device, device_id_type=MESH
    )


def to_lanes(column):
    rows = column.shape[0]
    return jnp.broadcast_to(column, (rows, rows)).T[:8]


def to_column(lanes):
    rows = lanes.shape[1]
    return jnp.broadcast_to(lanes[:1], (rows, rows)).T


def gather_kernel(
    n_seg, n_tp, mem_hbm, gain_ref, wk_hbm, wv_hbm,
    nt_hbm, k_ref, v_ref, scale_ref,
    buf, turned, wk, wv, kacc, vacc, mine, slots, scales, scol,
    mem_sem, w_sem, sq_tx, sq_rx, sc_tx, sc_rx, zr_tx, zl_tx, z_rx,
    seg_tx, seg_rx, sib_tx, sib_rx, out_sem,
):
    s = lax.axis_index("segment")
    t = lax.axis_index("tp")
    rows, cols = mem_hbm.shape
    half = rows // 2
    n_z = n_tp // 2
    hidden = n_tp * cols
    zi = t // 2
    core = t % 2
    own = pl.ds(pl.multiple_of(s * rows, rows), rows)
    load_m = pltpu.make_async_copy(mem_hbm, buf.at[t, own, :], mem_sem.at[0])
    load_k = pltpu.make_async_copy(wk_hbm, wk, w_sem.at[0])
    load_v = pltpu.make_async_copy(wv_hbm, wv, w_sem.at[1])
    load_m.start()

    few = jnp.minimum(zi, n_z - 1 - zi)

    def z_of(q):
        d = (q + 1) // 2
        near = jnp.where(q % 2 == 1, zi - d, zi + d)
        far = jnp.where(zi > n_z - 1 - zi, zi - (q - few), zi + (q - few))
        return jnp.where(q <= 2 * few, near, far)

    def block(q):
        return z_of(q) * 2 + core

    def piece(q, h, mask):
        start = pl.multiple_of((s ^ mask) * rows + h * half, half)
        return buf.at[block(q), pl.ds(start, half), :]

    def seg_copy(q, h, mask, b):
        ref = piece(q, h, mask)
        return remote(
            ref, ref, seg_tx.at[q, h, mask, b], seg_rx.at[q, h, mask ^ (1 << b)], (s ^ (1 << b), t)
        )

    def seg_arrival(q, h, mask):
        ref = piece(q, h, mask)
        b = bits_of(n_seg) - 1
        return remote(ref, ref, seg_tx.at[q, h, 0, b], seg_rx.at[q, h, mask], (s ^ (1 << b), t))

    def z_copy(z, to_right):
        ref = buf.at[z * 2 + core, own, :]
        if to_right:
            return remote(ref, ref, zr_tx.at[z], z_rx.at[z], (s, t + 2))
        return remote(ref, ref, zl_tx.at[z], z_rx.at[z], (s, t - 2))

    def z_each(q, act):
        z = z_of(q)

        @pl.when((z <= zi) & (zi + 1 < n_z))
        def _():
            act(z_copy(z, True))

        @pl.when((z >= zi) & (zi > 0))
        def _():
            act(z_copy(z, False))

    def z_arrival(q):
        z = z_of(q)
        ref = buf.at[z * 2 + core, own, :]
        return remote(ref, ref, zr_tx.at[z], z_rx.at[z], (s, t ^ 2))

    def sib_copy(q):
        ref = buf.at[block(q)]
        return remote(ref, ref, sib_tx.at[q], sib_rx.at[q], (s, t ^ 1))

    def sib_arrival(q):
        ref = buf.at[block(q) ^ 1]
        return remote(ref, ref, sib_tx.at[q], sib_rx.at[q], (s, t ^ 1))

    def out_copy(b):
        return pltpu.make_async_copy(turned.at[b], nt_hbm.at[b], out_sem.at[b])

    def sq_copy(m):
        return remote(mine, slots.at[m], sq_tx.at[m], sq_rx.at[m], (s, t ^ m))

    def sc_copy(m):
        return remote(scales.at[s], scales.at[s], sc_tx.at[m], sc_rx.at[m], (s ^ m, t))

    def sc_arrival(m):
        ref = scales.at[s ^ m]
        return remote(ref, ref, sc_tx.at[m], sc_rx.at[m], (s ^ m, t))

    relayed = []
    for h, order in enumerate(orders(n_seg)):
        have = [0]
        for b in order:
            for mask in have:
                if mask:
                    relayed.append((h, mask, b))
            have = have + [mask ^ (1 << b) for mask in have]
    waited = []
    for h, mask, _ in relayed:
        if (h, mask) not in waited:
            waited.append((h, mask))

    def first_sends(q):
        for h in range(2):
            for b in orders(n_seg)[h]:
                seg_copy(q, h, 0, b).start()

    def relay(q):
        seen = []
        for h, mask, b in relayed:
            if (h, mask) not in seen:
                seg_arrival(q, h, mask).wait_recv()
                seen.append((h, mask))
            seg_copy(q, h, mask, b).start()

    def project(b):
        rows_w = pl.ds(pl.multiple_of(b * cols, cols), cols)
        normed = (buf[b].astype(F32) * scol[:, :1] * gain_ref[b]).astype(BF16)
        turned[b] = normed.T
        out_copy(b).start()
        kacc[...] += jnp.dot(normed, wk[rows_w, :], preferred_element_type=F32)
        vacc[...] += jnp.dot(normed, wv[rows_w, :], preferred_element_type=F32)

    greet(n_seg, n_tp, s, t)
    load_m.wait()
    z_each(0, lambda c: c.start())
    first_sends(0)
    x = buf[t, own, :].astype(F32)
    mine[...] = to_lanes(jnp.sum(x * x, axis=1, keepdims=True))
    for m in range(1, n_tp):
        sq_copy(m).start()
    load_k.start()
    load_v.start()
    kacc[...] = jnp.zeros_like(kacc)
    vacc[...] = jnp.zeros_like(vacc)

    @pl.loop(0, n_z + 2)
    def _(i):
        @pl.when(i + 1 < n_z)
        def _():
            z_arrival(i + 1).wait_recv()
            z_each(i + 1, lambda c: c.start())
            first_sends(i + 1)

        @pl.when(i == 0)
        def _():
            total = mine[...]
            for m in range(1, n_tp):
                sq_copy(m).wait()
                total = total + slots[m]
            scales[s] = lax.rsqrt(total / hidden + EPS)
            for m in range(1, n_seg):
                sc_copy(m).start()

        @pl.when(i < n_z)
        def _():
            relay(i)

        @pl.when(i == 1)
        def _():
            for m in range(1, n_seg):
                sc_copy(m).wait_send()
                sc_arrival(m).wait_recv()
            for k in range(n_seg):
                scol[k * rows:(k + 1) * rows, :] = to_column(scales[k])[:, :128]
            load_k.wait()
            load_v.wait()

        @pl.when((i >= 1) & (i <= n_z))
        def _():
            for h in range(2):
                for mask in range(1, n_seg):
                    if (h, mask) not in waited:
                        seg_arrival(i - 1, h, mask).wait_recv()
            sib_copy(i - 1).start()

        @pl.when(i >= 2)
        def _():
            sib_arrival(i - 2).wait_recv()

        @pl.loop(jnp.where(i == 0, 2, jnp.where(i == 1, 1, 0)), jnp.where(i == n_z + 1, 1, 2))
        def _(j):
            project(block(i - 2 + j) ^ (1 - j))

    k_ref[...] = kacc[...].astype(BF16)
    v_ref[...] = vacc[...].astype(BF16)
    scale_ref[...] = scol[own, :]

    @pl.loop(0, n_z)
    def _(q):
        z_each(q, lambda c: c.wait_send())
        for h in range(2):
            for b in orders(n_seg)[h]:
                seg_copy(q, h, 0, b).wait_send()
        for h, mask, b in relayed:
            seg_copy(q, h, mask, b).wait_send()
        sib_copy(q).wait_send()
        out_copy(block(q)).wait()
        out_copy(block(q) ^ 1).wait()


def gather(n_seg, n_tp, memory, gain, wk, wv):
    rows, cols = memory.shape
    n_z = n_tp // 2
    nb = bits_of(n_seg)
    vmem = pl.BlockSpec(memory_space=pltpu.VMEM)
    anyw = pl.BlockSpec(memory_space=pl.ANY)
    src = n_seg * rows
    return pl.pallas_call(
        functools.partial(gather_kernel, n_seg, n_tp),
        out_shape=(
            jax.ShapeDtypeStruct((n_tp, cols, src), BF16),
            jax.ShapeDtypeStruct((src, cols), BF16),
            jax.ShapeDtypeStruct((src, cols), BF16),
            jax.ShapeDtypeStruct((rows, 128), F32),
        ),
        in_specs=[anyw, vmem, anyw, anyw],
        out_specs=(anyw, vmem, vmem, vmem),
        scratch_shapes=[
            VM((n_tp, src, cols), BF16),
            VM((n_tp, cols, src), BF16),
            VM(wk.shape, BF16),
            VM(wv.shape, BF16),
            VM((src, cols), F32),
            VM((src, cols), F32),
            VM((8, rows), F32),
            VM((n_tp, 8, rows), F32),
            VM((n_seg, 8, rows), F32),
            VM((src, 128), F32),
            DMA((1,)),
            DMA((2,)),
            DMA((n_tp,)),
            DMA((n_tp,)),
            DMA((n_seg,)),
            DMA((n_seg,)),
            DMA((n_z,)),
            DMA((n_z,)),
            DMA((n_z,)),
            DMA((n_z, 2, n_seg, nb)),
            DMA((n_z, 2, n_seg)),
            DMA((n_z,)),
            DMA((n_z,)),
            DMA((n_tp,)),
        ],
        compiler_params=pltpu.CompilerParams(collective_id=0, has_side_effects=True),
        name="gather_project",
    )(memory, gain, wk, wv)


def attention_kernel(q_ref, k_ref, v_ref, d_ref, c_ref, qg_ref, gk_ref, gv_ref, gk_acc, gv_acc):
    i = pl.program_id(1)
    scale = HD ** (-0.5)
    nt = (((1,), (1,)), ((), ()))
    tn = (((0,), (0,)), ((), ()))
    q, k, v, d = q_ref[...], k_ref[...], v_ref[...], d_ref[...]
    scores = lax.dot_general(q, k, nt, preferred_element_type=F32) * scale
    grad_attend = lax.dot_general(d, v, nt, preferred_element_type=F32)
    exponent = jnp.exp(scores - jnp.max(scores, axis=-1, keepdims=True))
    attend = exponent * (1.0 / jnp.sum(exponent, axis=-1, keepdims=True))
    attend_low = attend.astype(BF16)
    row_dots = jnp.sum(grad_attend * attend, axis=-1, keepdims=True)
    grad_scores = (attend * (grad_attend - row_dots) * scale).astype(BF16)
    c_ref[...] = jnp.dot(attend_low, v, preferred_element_type=F32).astype(BF16)
    qg_ref[...] = jnp.dot(grad_scores, k, preferred_element_type=F32).astype(BF16)
    gk = lax.dot_general(grad_scores, q, tn, preferred_element_type=F32)
    gv = lax.dot_general(attend_low, d, tn, preferred_element_type=F32)

    @pl.when(i == 0)
    def _():
        gk_acc[...] = gk
        gv_acc[...] = gv

    @pl.when(i > 0)
    def _():
        gk_acc[...] += gk
        gv_acc[...] += gv

    @pl.when(i == pl.num_programs(1) - 1)
    def _():
        gk_ref[...] = gk_acc[...].astype(BF16)
        gv_ref[...] = gv_acc[...].astype(BF16)


def attention(q, k, v, d):
    tgt, cols = q.shape
    src = k.shape[0]
    tile = tgt
    tspec = pl.BlockSpec((tile, HD), lambda h, i: (i, h))
    sspec = pl.BlockSpec((src, HD), lambda h, i: (0, h))
    return pl.pallas_call(
        attention_kernel,
        grid=(cols // HD, tgt // tile),
        out_shape=(
            jax.ShapeDtypeStruct((tgt, cols), BF16),
            jax.ShapeDtypeStruct((tgt, cols), BF16),
            jax.ShapeDtypeStruct((src, cols), BF16),
            jax.ShapeDtypeStruct((src, cols), BF16),
        ),
        in_specs=[tspec, sspec, sspec, tspec],
        out_specs=(tspec, tspec, sspec, sspec),
        scratch_shapes=[VM((src, HD), F32), VM((src, HD), F32)],
        name="attention",
    )(q, k, v, d)


def weight_grad_kernel(n_ref, gk_ref, gv_ref, kg_ref, vg_ref):
    kg_ref[...] = jnp.dot(n_ref[...], gk_ref[...], preferred_element_type=F32)
    vg_ref[...] = jnp.dot(n_ref[...], gv_ref[...], preferred_element_type=F32)


def weight_grads(normed, gk, gv):
    n_tp, cols, src = normed.shape
    tile = 2 * cols
    full = pl.BlockSpec((src, cols), lambda i: (0, 0))
    out = pl.BlockSpec((tile, cols), lambda i: (i, 0))
    return pl.pallas_call(
        weight_grad_kernel,
        grid=(n_tp * cols // tile,),
        out_shape=(jax.ShapeDtypeStruct((n_tp * cols, cols), F32),) * 2,
        in_specs=[pl.BlockSpec((tile, src), lambda i: (i, 0)), full, full],
        out_specs=(out, out),
        name="weight_grads",
    )(normed.reshape(n_tp * cols, src), gk, gv)


def scatter_kernel(
    n_seg, n_tp, gk_ref, gv_ref, k_ref, v_ref, wk_hbm, wv_hbm, mem_ref, gain_ref, scale_ref,
    out_ref,
    wk, wv, sib_out, sib_in, own, seg_in, z_in, mine, slots, sums, parts,
    wk_sem, wv_sem, sq_tx, sq_rx, in_tx, in_rx, z_tx, z_rx, seg_tx, seg_rx, sib_tx, sib_rx,
):
    s = lax.axis_index("segment")
    t = lax.axis_index("tp")
    rows, cols = mem_ref.shape
    half = rows // 2
    n_z = n_tp // 2
    hidden = n_tp * cols
    nt = (((1,), (1,)), ((), ()))

    def block(i):
        return t ^ ((n_z - 1 - i) * 2)

    def load(b, i):
        r = pl.ds(pl.multiple_of(b * cols, cols), cols)
        return (
            pltpu.make_async_copy(wk_hbm.at[r, :], wk.at[i], wk_sem.at[i]),
            pltpu.make_async_copy(wv_hbm.at[r, :], wv.at[i], wv_sem.at[i]),
        )

    @pl.loop(0, n_z)
    def _(i):
        for j in range(2):
            for c in load(block(i) ^ (1 - j), i * 2 + j):
                c.start()

    greet(n_seg, n_tp, s, t)

    def sq_copy(m):
        return remote(mine, slots.at[m], sq_tx.at[m], sq_rx.at[m], (s, t ^ m))

    def in_copy(m):
        return remote(sums.at[s ^ m], parts.at[m], in_tx.at[m], in_rx.at[m], (s ^ m, t))

    for k in range(n_seg):
        r = slice(k * rows, (k + 1) * rows)
        both = gk_ref[r].astype(F32) * k_ref[r].astype(F32) + gv_ref[r].astype(F32) * v_ref[
            r
        ].astype(F32)
        mine[k] = to_lanes(jnp.sum(both, axis=1, keepdims=True))
    for m in range(1, n_tp):
        sq_copy(m).start()

    def product(i):
        return lax.dot_general(
            gk_ref[...], wk[i], nt, preferred_element_type=F32
        ) + lax.dot_general(gv_ref[...], wv[i], nt, preferred_element_type=F32)

    def sib_copy(i):
        return remote(sib_out.at[i], sib_in.at[i], sib_tx.at[i], sib_rx.at[i], (s, t ^ 1))

    def rows_of(mask, h):
        return pl.ds(pl.multiple_of((s ^ mask) * rows + h * half, half), half)

    def seg_copy(i, h, mask, b):
        return remote(
            own.at[i, rows_of(mask, h), :],
            seg_in.at[i, h, mask],
            seg_tx.at[i, h, mask],
            seg_rx.at[i, h, mask],
            (s ^ (1 << b), t),
        )

    def z_copy(i):
        m = n_z - 1 - i
        r = pl.ds(pl.multiple_of(s * rows, rows), rows)
        return remote(own.at[i, r, :], z_in.at[i], z_tx.at[i], z_rx.at[i], (s, t ^ (m * 2)))

    steps = []
    for j in range(bits_of(n_seg)):
        pair = []
        for order in orders(n_seg):
            done = sum(1 << b for b in order[:j])
            b = order[j]
            pair.append((b, [k for k in range(n_seg) if not (k & done) and (k >> b) & 1]))
        steps.append(pair)

    def send(i, j):
        for h in range(2):
            b, masks = steps[j][h]
            for mask in masks:
                seg_copy(i, h, mask, b).start()

    def receive(i, j):
        for h in range(2):
            b, masks = steps[j][h]
            for mask in masks:
                seg_copy(i, h, mask, b).wait_recv()
                r = rows_of(mask ^ (1 << b), h)
                own[i, r, :] = (
                    own[i, r, :].astype(F32) + seg_in[i, h, mask].astype(F32)
                ).astype(BF16)

    n_steps = len(steps)

    @pl.loop(0, n_z + n_steps + 1)
    def _(i):
        @pl.when(i < n_z)
        def _():
            for c in load(block(i) ^ 1, i * 2):
                c.wait()
            sib_out[i] = product(i * 2).astype(BF16)
            sib_copy(i).start()

        @pl.when((i > 0) & (i <= n_z))
        def _():
            k = i - 1
            for c in load(block(k), k * 2 + 1):
                c.wait()
            mine_part = product(k * 2 + 1)
            sib_copy(k).wait_recv()
            own[k] = (mine_part + sib_in[k].astype(F32)).astype(BF16)
            send(k, 0)

        @pl.when(i == 2)
        def _():
            total = mine[...]
            for m in range(1, n_tp):
                sq_copy(m).wait()
                total = total + slots[m]
            sums[...] = total
            for m in range(1, n_seg):
                in_copy(m).start()

        for j in range(n_steps):
            k = i - 2 - j

            @pl.when((k >= 0) & (k < n_z))
            def _():
                receive(k, j)
                if j + 1 < n_steps:
                    send(k, j + 1)
                else:
                    @pl.when(k < n_z - 1)
                    def _():
                        z_copy(k).start()

    own_rows = pl.ds(pl.multiple_of(s * rows, rows), rows)
    total = own[n_z - 1, own_rows, :].astype(F32)
    for i in range(n_z - 1):
        z_copy(i).wait_recv()
        total = total + z_in[i].astype(F32)
    upper = total * gain_ref[t]
    scale = scale_ref[:, :1]
    xhat = mem_ref[...].astype(F32) * scale
    inner = sums[s]
    for m in range(1, n_seg):
        in_copy(m).wait()
        inner = inner + parts[m]
    inner = to_column(inner)[:, :1]
    out_ref[...] = scale * (upper - xhat * (inner / hidden))

    for i in range(n_z - 1):
        z_copy(i).wait_send()

    @pl.loop(0, n_z)
    def _(i):
        sib_copy(i).wait_send()
        for j in range(n_steps):
            for h in range(2):
                b, masks = steps[j][h]
                for mask in masks:
                    seg_copy(i, h, mask, b).wait_send()


def scatter(n_seg, n_tp, gk, gv, key_rows, value_rows, wk, wv, memory, gain, scale):
    rows, cols = memory.shape
    n_z = n_tp // 2
    vmem = pl.BlockSpec(memory_space=pltpu.VMEM)
    anyw = pl.BlockSpec(memory_space=pl.ANY)
    src = n_seg * rows
    return pl.pallas_call(
        functools.partial(scatter_kernel, n_seg, n_tp),
        out_shape=jax.ShapeDtypeStruct((rows, cols), F32),
        in_specs=[vmem, vmem, vmem, vmem, anyw, anyw, vmem, vmem, vmem],
        out_specs=vmem,
        scratch_shapes=[
            VM((n_tp, cols, cols), BF16),
            VM((n_tp, cols, cols), BF16),
            VM((n_z, src, cols), BF16),
            VM((n_z, src, cols), BF16),
            VM((n_z, src, cols), BF16),
            VM((n_z, 2, n_seg, rows // 2, cols), BF16),
            VM((n_z, rows, cols), BF16),
            VM((n_seg, 8, rows), F32),
            VM((n_tp, n_seg, 8, rows), F32),
            VM((n_seg, 8, rows), F32),
            VM((n_seg, 8, rows), F32),
            DMA((n_tp,)),
            DMA((n_tp,)),
            DMA((n_tp,)),
            DMA((n_tp,)),
            DMA((n_seg,)),
            DMA((n_seg,)),
            DMA((n_z,)),
            DMA((n_z,)),
            DMA((n_z, 2, n_seg)),
            DMA((n_z, 2, n_seg)),
            DMA((n_z,)),
            DMA((n_z,)),
        ],
        compiler_params=pltpu.CompilerParams(collective_id=1, has_side_effects=True),
        name="grad_scatter",
    )(gk, gv, key_rows, value_rows, wk, wv, memory, gain, scale)


def local(n_seg, n_tp, memory, norm_gain, queries, key_weight, value_weight, context_grad):
    wk, wv = key_weight[0], value_weight[0]
    gain = norm_gain.reshape(n_tp, 1, memory.shape[1])
    normed, key_rows, value_rows, scale = gather(n_seg, n_tp, memory, gain, wk, wv)
    context, query_grad, gk, gv = attention(queries[0], key_rows, value_rows, context_grad[0])
    key_grad, value_grad = weight_grads(normed, gk, gv)
    out = scatter(n_seg, n_tp, gk, gv, key_rows, value_rows, wk, wv, memory, gain, scale)
    return context[None], query_grad[None], key_grad[None], value_grad[None], out


def solution(mesh):
    section = P("segment", None, "tp")
    n_seg, n_tp = mesh.shape["segment"], mesh.shape["tp"]
    return jax.shard_map(
        functools.partial(local, n_seg, n_tp),
        mesh=mesh,
        in_specs=(P("segment", "tp"), P(), section, section, section, section),
        out_specs=(section, section, section, section, P("segment", "tp")),
        check_vma=False,
    )
```
